32 devices in a mesh: groups: 2 (over x), gx: 8 (over z, y), gy: 2 (over core).
Axes of the slice: x: 2, y: 2, z: 4, core: 2. Of those that a mesh axis runs over, the one named last changes fastest.
Arguments:
- initial_voltage: float32 [256, 128, 256], P(('groups', 'gx'), 'gy'), parts along dimension 0, may hold values from -0.1 to 1.1
- conductivity: float32 [256, 128, 256], P(('groups', 'gx'), 'gy'), parts along dimension 0, may hold values from 0.3 to 1.2
- tissue_mask: int32 [256, 128, 256], P(('groups', 'gx'), 'gy'), parts along dimension 0, may hold values 0 or 1
- target_step: int32 [256, 128, 256], P(('groups', 'gx'), 'gy'), parts along dimension 0, may hold values from 0 to 8
- initial_purkinje: float32 [16384, 128], P(('groups', 'gx', 'gy')), parts along dimension 0, may hold values from -0.1 to 1.1
- purkinje_conductivity: float32 [16384], P(('groups', 'gx', 'gy')), parts along dimension 0, may hold values from 0.5 to 4
- segment_parent: int32 [16384], P(('groups', 'gx', 'gy')), parts along dimension 0, may hold values from -1 to 8190, as said below
- purkinje_target: int32 [16384, 128], P(('groups', 'gx', 'gy')), parts along dimension 0, may hold values from 0 to 8
- junction_voxel: int32 [16384], P(('groups', 'gx', 'gy')), parts along dimension 0, may hold values from 0 to 4194303, as said below
- junction_node: int32 [16384], P(('groups', 'gx', 'gy')), parts along dimension 0, may hold values from 0 to 1048575, as said below
Outputs:
- final_voltage: float32 [256, 128, 256], P(('groups', 'gx'), 'gy'), parts along dimension 0
- final_purkinje: float32 [16384, 128], P(('groups', 'gx', 'gy')), parts along dimension 0
- conductivity_gradient: float32 [256, 128, 256], P(('groups', 'gx'), 'gy'), parts along dimension 0
- purkinje_gradient: float32 [16384], P(('groups', 'gx', 'gy')), parts along dimension 0
- voltage_adjoint: float32 [256, 128, 256], P(('groups', 'gx'), 'gy'), parts along dimension 0
- purkinje_adjoint: float32 [16384, 128], P(('groups', 'gx', 'gy')), parts along dimension 0
The draws below stay inside these ranges and needn't reach their ends.
There are 2 independent parts, one for each index of `groups`. The reference program is written for one: setup_inputs(seed, part) draws one part's arguments, and reference() takes and returns one part's arrays. A program takes and returns all parts, laid end to end along the dimension named above; each array names one. Nothing has to cross between parts.
Inputs may be any that keep to these rules, and one draw needn't show every extreme that they name: `junction_voxel`: A flat voxel index (x * 128 + y) * 256 + z. Among the 512 entries of one device's block, at most 64 lie in the voxel block of one tissue device, and some tissue device holds exactly 64 junctions of every device's block. `junction_node`: A flat node index s * 128 + i; the segment s of entry k lies in the same device block as entry k (block k // 512). `segment_parent`: -1 marks a root; otherwise the number of an earlier segment, at most 1024 before it.
All inputs are finite; a program needn't handle non-finite values. No bound on the sum of `tissue_mask` on one device may be relied on, other than what follows from the above.
Results may differ from the reference program's by a relative error of at most 0.0001.
Values sent between devices are 32-bit elements; how exact they have to be, the bound alone decides.
A program may use at most 128 MiB of HBM per device.

```python
import math
import jax
import jax.numpy as jnp
from jax import lax

CX = 16
CY = 64
CZ = 256
SPD = 512
SEG = 128
JPD = 512
NX = 128
NY = 128
NSEG = 8192
CAP = 64
N_GX = 8
N_GY = 2


def junction_plan(key):
    folded = jax.random.fold_in(key, 4242)
    subkeys = jax.random.split(folded, 6)
    devices = N_GX * N_GY
    slot_count = devices * CAP
    ranking = jax.random.permutation(subkeys[0], devices)
    priority = jnp.where(ranking < 2, 3, jnp.where(ranking < 2 + devices // 8, 2, jnp.where(ranking < devices // 2, 1, 0)))
    slot_number = jnp.arange(slot_count, dtype=jnp.int32)
    slot_device = slot_number // CAP
    jitter = jax.random.randint(subkeys[1], (devices, slot_count), 0, 4096)
    scores = (priority[slot_device][None, :] * 4096 + jitter) * slot_count + slot_number[None, :]
    chosen = jnp.sort(lax.top_k(scores, JPD)[1], axis=1)
    target = chosen // CAP
    offset_first = jax.random.randint(subkeys[2], (devices, JPD), 0, CX)
    offset_second = jax.random.randint(subkeys[3], (devices, JPD), 0, CY)
    offset_third = jax.random.randint(subkeys[4], (devices, JPD), 0, CZ)
    coord_first = target // N_GY * CX + offset_first
    coord_second = target % N_GY * CY + offset_second
    voxel_index = (coord_first * NY + coord_second) * CZ + offset_third
    source = jnp.arange(devices, dtype=jnp.int32)[:, None]
    purkinje_node = source * (SPD * SEG) + jax.random.randint(subkeys[5], (devices, JPD), 0, SPD * SEG)
    return (voxel_index.reshape(-1).astype(jnp.int32), purkinje_node.reshape(-1).astype(jnp.int32))


def draw_junction_voxel(key, part):
    return junction_plan(key)[0]


def draw_junction_node(key, part):
    return junction_plan(key)[1]


def draw_segment_parent(key, part):
    folded = jax.random.fold_in(key, 777)
    number = jnp.arange(NSEG, dtype=jnp.int32)
    distance = jax.random.randint(folded, (NSEG,), 1, 2 * SPD + 1)
    earlier = number - distance
    return jnp.where(earlier < 0, -1, earlier).astype(jnp.int32)


def set_ends(array, own_key, smallest, largest):
    shape = array.shape
    spot = [jax.random.randint(jax.random.fold_in(own_key, axis), (), 0, shape[axis]) for axis in range(len(shape))]
    array = array.at[tuple(spot)].set(smallest)
    longest = shape.index(max(shape))
    spot[longest] = (spot[longest] + 1) % shape[longest]
    return array.at[tuple(spot)].set(largest)


def block_scale(own_key, extent, shards, least, top_value):
    loudness = 1.0
    for dim, shards_of in shards:
        steps = jax.random.uniform(jax.random.fold_in(jax.random.fold_in(own_key, 6), dim), (shards_of,), jnp.float32, least / len(shards), top_value / len(shards))
        loudness = loudness * jnp.repeat(jnp.exp(steps), extent[dim] // shards_of).reshape((-1,) + (1,) * (len(extent) - 1 - dim))
    return loudness


def setup_inputs(seed: int = 0, part: int = 0) -> dict:
    splits = jax.random.split(jax.random.key(seed), 11)
    part_keys = jax.random.split(jax.random.fold_in(splits[10], part), 11)
    initial_voltage = jnp.clip(-0.1 + 1.2 * jax.random.uniform(part_keys[0], (NX, NY, CZ), jnp.float32) ** block_scale(part_keys[0], (NX, NY, CZ), ((0, 8), (1, 2)), -0.2, 0.2), -0.1, 1.1)
    conductivity = jnp.clip(jnp.exp(math.log(1.2) - 1.3862944 * jax.random.uniform(part_keys[1], (NX, NY, CZ), jnp.float32) ** block_scale(part_keys[1], (NX, NY, CZ), ((0, 8), (1, 2)), -0.2, 0.2)), 0.3, 1.2)
    tissue_mask = set_ends((jax.random.randint(part_keys[2], (NX, NY, CZ), 0, 8) < 7).astype(jnp.int32), jax.random.fold_in(part_keys[2], 1), 0, 1)
    target_step = set_ends(jax.random.randint(part_keys[3], (NX, NY, CZ), 0, 9), jax.random.fold_in(part_keys[3], 1), 0, 8).astype(jnp.int32)
    initial_purkinje = jnp.clip(-0.1 + 1.2 * jax.random.uniform(part_keys[4], (NSEG, SEG), jnp.float32) ** block_scale(part_keys[4], (NSEG, SEG), ((0, 16),), -0.2, 0.2), -0.1, 1.1)
    purkinje_conductivity = jnp.clip(jnp.exp(math.log(4.0) - 2.0794415 * jax.random.uniform(part_keys[5], (NSEG,), jnp.float32) ** block_scale(part_keys[5], (NSEG,), ((0, 16),), -0.2, 0.2)), 0.5, 4.0)
    segment_parent = draw_segment_parent(jax.random.fold_in(jax.random.fold_in(splits[10], part), 71), part)
    purkinje_target = set_ends(jax.random.randint(part_keys[7], (NSEG, SEG), 0, 9), jax.random.fold_in(part_keys[7], 1), 0, 8).astype(jnp.int32)
    junction_voxel = draw_junction_voxel(jax.random.fold_in(jax.random.fold_in(splits[10], part), 71), part)
    junction_node = draw_junction_node(jax.random.fold_in(jax.random.fold_in(splits[10], part), 71), part)
    return {"initial_voltage": initial_voltage, "conductivity": conductivity, "tissue_mask": tissue_mask, "target_step": target_step, "initial_purkinje": initial_purkinje, "purkinje_conductivity": purkinje_conductivity, "segment_parent": segment_parent, "purkinje_target": purkinje_target, "junction_voxel": junction_voxel, "junction_node": junction_node}


time_step = 0.05
gap_conductance = 4.0
ion_rate = 8.0
threshold = 0.15
loss_weight = 10.0
target_span = 8.0


def ionic(values):
    return ion_rate * values * (values - threshold) * (1.0 - values)


def slope(values):
    return ion_rate * (-3.0 * values * values + 2.0 * (1.0 + threshold) * values - threshold)


def neighbours(padded):
    return [padded[2:, 1:-1, 1:-1], padded[:-2, 1:-1, 1:-1], padded[1:-1, 2:, 1:-1],
            padded[1:-1, :-2, 1:-1], padded[1:-1, 1:-1, 2:], padded[1:-1, 1:-1, :-2]]


def cable(values, gains, safe_parent, has_parent):
    difference = values[:, 1:] - values[:, :-1]
    edge_flux = gains[:, None] * difference
    result = jnp.pad(edge_flux, ((0, 0), (0, 1))) - jnp.pad(edge_flux, ((0, 0), (1, 0)))
    parent_tail = values[safe_parent, -1]
    head_flux = jnp.where(has_parent, gains * (parent_tail - values[:, 0]), 0.0)
    tail_inflow = jnp.zeros(values.shape[0], values.dtype).at[safe_parent].add(-head_flux)
    result = result.at[:, 0].add(head_flux).at[:, -1].add(tail_inflow)
    return result, parent_tail


def junction(tissue_values, cable_values, junction_voxel, junction_node):
    tissue_at = tissue_values.reshape(-1)[junction_voxel]
    cable_at = cable_values.reshape(-1)[junction_node]
    current = gap_conductance * (cable_at - tissue_at)
    into_tissue = jnp.zeros(tissue_values.size, tissue_values.dtype).at[junction_voxel].add(current)
    into_cable = jnp.zeros(cable_values.size, cable_values.dtype).at[junction_node].add(current)
    return into_tissue.reshape(tissue_values.shape), into_cable.reshape(cable_values.shape)


def reference(initial_voltage, conductivity, tissue_mask, target_step, initial_purkinje,
              purkinje_conductivity, segment_parent, purkinje_target, junction_voxel, junction_node):
    mask_float = tissue_mask.astype(jnp.float32)
    sigma_beside = neighbours(jnp.pad(conductivity, 1))
    mask_beside = neighbours(jnp.pad(mask_float, 1))
    conduct = [0.5 * (conductivity + other_sigma) * mask_float * other_mask
               for other_sigma, other_mask in zip(sigma_beside, mask_beside)]
    halves = [0.5 * mask_float * other_mask for other_mask in mask_beside]
    has_parent = segment_parent >= 0
    parent_float = has_parent.astype(jnp.float32)
    safe_parent = jnp.where(has_parent, segment_parent, 0).astype(jnp.int32)

    def tissue_apply(values):
        beside = neighbours(jnp.pad(values, 1))
        total = jnp.zeros_like(values)
        for weight, other in zip(conduct, beside):
            total = total + weight * (other - values)
        return total, beside

    voltage = initial_voltage
    purkinje = initial_purkinje
    history = []
    for repeat in range(2):
        flux_tissue, beside = tissue_apply(voltage)
        flux_cable, parent_tail = cable(purkinje, purkinje_conductivity, safe_parent, has_parent)
        into_tissue, into_cable = junction(voltage, purkinje, junction_voxel, junction_node)
        history.append((voltage, purkinje, beside, parent_tail))
        voltage, purkinje = (voltage + time_step * (flux_tissue + ionic(voltage) + into_tissue),
                             purkinje + time_step * (flux_cable + ionic(purkinje) - into_cable))
    adjoint_voltage = loss_weight * mask_float * (voltage - (1.0 - target_step.astype(jnp.float32) / target_span))
    adjoint_cable = loss_weight * (purkinje - (1.0 - purkinje_target.astype(jnp.float32) / target_span))
    grad_sigma = jnp.zeros_like(voltage)
    grad_cable = jnp.zeros_like(purkinje_conductivity)
    for state in reversed(history):
        old_voltage, old_purkinje, old_beside, old_tail = state
        flux_tissue, adjoint_beside = tissue_apply(adjoint_voltage)
        flux_cable, adjoint_tail = cable(adjoint_cable, purkinje_conductivity, safe_parent, has_parent)
        into_tissue, into_cable = junction(adjoint_voltage, adjoint_cable, junction_voxel, junction_node)
        total = jnp.zeros_like(voltage)
        for half, other_adjoint, other_voltage in zip(halves, adjoint_beside, old_beside):
            total = total + half * (adjoint_voltage - other_adjoint) * (other_voltage - old_voltage)
        grad_sigma = grad_sigma + time_step * total
        inner = jnp.sum((adjoint_cable[:, :-1] - adjoint_cable[:, 1:]) * (old_purkinje[:, 1:] - old_purkinje[:, :-1]), axis=1)
        head = parent_float * (adjoint_cable[:, 0] - adjoint_tail) * (old_tail - old_purkinje[:, 0])
        grad_cable = grad_cable + time_step * (inner + head)
        adjoint_voltage, adjoint_cable = (
            adjoint_voltage + time_step * (flux_tissue + slope(old_voltage) * adjoint_voltage + into_tissue),
            adjoint_cable + time_step * (flux_cable + slope(old_purkinje) * adjoint_cable - into_cable))
    return voltage, purkinje, grad_sigma, grad_cable, adjoint_voltage, adjoint_cable
```

```python
import functools

import jax
import jax.numpy as jnp
from jax import lax
from jax.experimental import pallas as pl
from jax.experimental.pallas import tpu as pltpu
from jax.sharding import PartitionSpec as P

time_step = 0.05
gap_conductance = 4.0
ion_rate = 8.0
threshold = 0.15
loss_weight = 10.0
target_span = 8.0
LANES = 128
F32 = jnp.float32
BF16 = jnp.bfloat16


def ionic(values):
    return ion_rate * values * (values - threshold) * (1.0 - values)


def slope(values):
    return ion_rate * (-3.0 * values * values + 2.0 * (1.0 + threshold) * values - threshold)


def pieces(values):
    high = values.astype(BF16)
    return high, (values - high.astype(F32)).astype(BF16)


def dot(a, b):
    return lax.dot_general(a, b, (((1,), (0,)), ((), ())), preferred_element_type=F32)


def kernel(
    grid_x, grid_y, cap,
    v0_h, sigma_h, mask_h, target_h, y0_h, sigma_row, parent_row, ptarget_h, slot_voxel, slot_node,
    v2_o, y2_o, gs_o, gp_o, la_o, mu_o,
    vp, hys, hyr, tmp_mask, target, gxf, gym, gyp, gzm, gzp, v2b, l0b, gsb,
    ys, y2b, mu0b, ptarget, pb, sb, ptb, pgb,
    ot, ott, lm, xs, ws, op, opt, lmp, yss, wps,
    qt, qp, ta, tb, colb, colp, send, recv, voxr,
    tails, heads, tailr, headr, kids, kidr,
    loc_sem, js, jr, vs, vr, xs_s, xs_r, ysm_s, ysm_r, cs_s, cs_r, ks_s, ks_r,
):
    D = grid_x * grid_y
    cx, cy, cz = v2b.shape
    S, N = y2b.shape
    slots = D * cap
    rows = cx * cy
    gx = lax.axis_index("gx")
    gy = lax.axis_index("gy")
    me = gx * grid_y + gy

    def dev(flat):
        return {"gx": lax.div(flat, grid_y), "gy": lax.rem(flat, grid_y)}

    def rc(src, dst, s, r, where):
        return pltpu.make_async_remote_copy(
            src_ref=src, dst_ref=dst, send_sem=s, recv_sem=r,
            device_id=where, device_id_type=pl.DeviceIdType.MESH,
        )

    loads = [
        pltpu.make_async_copy(v0_h, vp.at[0, pl.ds(1, cx)], loc_sem.at[0]),
        pltpu.make_async_copy(sigma_h, gsb, loc_sem.at[1]),
        pltpu.make_async_copy(mask_h, tmp_mask, loc_sem.at[2]),
        pltpu.make_async_copy(y0_h, ys.at[0], loc_sem.at[3]),
        pltpu.make_async_copy(target_h, target, loc_sem.at[4]),
        pltpu.make_async_copy(ptarget_h, ptarget, loc_sem.at[5]),
    ]
    for c in loads:
        c.start()

    barrier = pltpu.get_barrier_semaphore()

    def greet(o, _):
        pl.semaphore_signal(
            barrier, inc=1, device_id=dev(lax.rem(me + o, D)), device_id_type=pl.DeviceIdType.MESH
        )
        return 0

    lax.fori_loop(1, D, greet, 0)
    kids[0:1, :] = sigma_row[...]
    kids[1:2, :] = parent_row[...]
    pl.semaphore_wait(barrier, D - 1)

    def vox_copy(o):
        to = lax.rem(me + o, D)
        return rc(slot_voxel.at[to], voxr.at[me], vs.at[o], vr.at[o], dev(to))

    def junction_copy(k, o):
        to = lax.rem(me + o, D)
        return rc(send.at[k, to], recv.at[k, me], js.at[k, o], jr.at[k, o], dev(to))

    def over_partners(make, act):
        def step(o, _):
            act(make(o))
            return 0

        lax.fori_loop(1, D, step, 0)

    def kid_copy(j):
        return rc(kids, kidr.at[j - 1], ks_s.at[j - 1], ks_r.at[j - 1], dev(lax.rem(me + D - j, D)))

    def cable_copies(k):
        out = []
        for j in (1, 2):
            out.append(rc(tails.at[k], tailr.at[k, j - 1], cs_s.at[k, j - 1], cs_r.at[k, j - 1],
                          dev(lax.rem(me + j, D))))
            out.append(rc(heads.at[k], headr.at[k, j - 1], cs_s.at[k, j + 1], cs_r.at[k, j + 1],
                          dev(lax.rem(me + D - j, D))))
        return out

    def up_copy(k):
        return rc(vp.at[k, cx], vp.at[k, 0], xs_s.at[k, 0], xs_r.at[k, 0],
                  {"gx": lax.rem(gx + 1, grid_x), "gy": gy})

    def down_copy(k):
        return rc(vp.at[k, 1], vp.at[k, cx + 1], xs_s.at[k, 1], xs_r.at[k, 1],
                  {"gx": lax.rem(gx + grid_x - 1, grid_x), "gy": gy})

    def side_copy(k):
        return rc(hys.at[k], hyr.at[k], ysm_s.at[k], ysm_r.at[k], {"gx": gx, "gy": 1 - gy})

    def halo_start(k):
        @pl.when(gx < grid_x - 1)
        def _():
            up_copy(k).start()

        @pl.when(gx > 0)
        def _():
            down_copy(k).start()

        side_copy(k).start()

    def halo_wait(k):
        @pl.when(gx > 0)
        def _():
            up_copy(k).wait_recv()

        @pl.when(gx < grid_x - 1)
        def _():
            down_copy(k).wait_recv()

        side_copy(k).wait_recv()

    def halo_sent(k):
        @pl.when(gx < grid_x - 1)
        def _():
            up_copy(k).wait_send()

        @pl.when(gx > 0)
        def _():
            down_copy(k).wait_send()

        side_copy(k).wait_send()

    over_partners(vox_copy, lambda c: c.start())
    for j in (1, 2):
        kid_copy(j).start()
    voxr[me] = slot_voxel[me]

    zero_plane = jnp.zeros((cy, cz), F32)

    @pl.when(gx == 0)
    def _():
        for k in range(5):
            vp[k, 0] = zero_plane

    @pl.when(gx == grid_x - 1)
    def _():
        for k in range(5):
            vp[k, cx + 1] = zero_plane

    def split_plane(i, c):
        high, low = pieces(c)
        at = pl.ds(pl.multiple_of(i * cy, cy), cy)
        xs[at, 0:cz] = high
        xs[at, cz : 2 * cz] = low

    def edge_row(c):
        return jnp.where(gy == 0, c[cy - 1 : cy, :], c[0:1, :])

    for n in range(4):
        loads[n].wait()

    def prepare(i, _):
        masked = gsb[i] * tmp_mask[i].astype(F32)
        vp[4, i + 1] = masked
        hys[4, pl.ds(i, 1), :] = edge_row(masked)
        c = vp[0, i + 1]
        hys[0, pl.ds(i, 1), :] = edge_row(c)
        split_plane(i, c)
        return 0

    lax.fori_loop(0, cx, prepare, 0)
    halo_start(0)
    halo_start(4)

    def cable_start(k):
        y = ys[k]
        turned = jnp.transpose(y)
        tails[k] = turned[N - 1 : N, :]
        heads[k] = turned[0:1, :]
        for c in cable_copies(k):
            c.start()
        high, low = pieces(y)
        yss[:, 0:N] = high
        yss[:, N : 2 * N] = low

    cable_start(0)
    pb[...] = jnp.transpose(jnp.broadcast_to(parent_row[...], (LANES, S)))
    sb[...] = jnp.transpose(jnp.broadcast_to(sigma_row[...], (LANES, S)))
    pgb[...] = jnp.zeros_like(pgb)

    def build(source, width, depth, onehot, onehot_t, lane_mask, column):
        ta[...] = jnp.zeros_like(ta)
        for d in range(D):
            ta[d : d + 1, :] = source[d]
        index = jnp.transpose(ta[...])[:cap, :]
        row = jnp.floor(index * (1.0 / width))
        lane = index - row * width
        lane_of = lax.broadcasted_iota(jnp.int32, (1, width), 1).astype(F32)
        row_of = lax.broadcasted_iota(jnp.int32, (1, depth), 1).astype(F32)
        for d in range(D):
            at = slice(d * cap, (d + 1) * cap)
            r = row[:, d : d + 1]
            onehot[at, :] = jnp.where(r == row_of, 1.0, 0.0).astype(BF16)
            lane_mask[at, :] = jnp.where(lane[:, d : d + 1] == lane_of, 1.0, 0.0)
            column[at, :] = jnp.broadcast_to(r, (cap, LANES))
        row_line = jnp.transpose(column[...])[0:1, :]
        step = 64

        def fill(b, _):
            ids = (lax.broadcasted_iota(jnp.int32, (step, 1), 0) + b * step).astype(F32)
            onehot_t[pl.ds(pl.multiple_of(b * step, step), step), :] = jnp.where(
                ids == row_line, 1.0, 0.0
            ).astype(BF16)
            return 0

        lax.fori_loop(0, depth // step, fill, 0)

    build(slot_node, N, S, op, opt, lmp, colp)
    over_partners(vox_copy, lambda c: c.wait_recv())
    build(voxr, cz, rows, ot, ott, lm, colb)

    lane_id = lax.broadcasted_iota(jnp.int32, (1, LANES), 1)
    block = min(slots, 512)
    per_block = block // cap
    qt[...] = jnp.zeros_like(qt)
    qp[...] = jnp.zeros_like(qp)

    def gather(k):
        def step(b, carry):
            tissue, cable = carry
            at = pl.ds(pl.multiple_of(b * block, block), block)
            got = dot(ot[at, :], xs[...])
            got = (got[:, :cz] + got[:, cz:]) * lm[at, :]
            line = jnp.sum(got, axis=1, keepdims=True)
            gop = dot(op[at, :], yss[...])
            gop = (gop[:, :N] + gop[:, N:]) * lmp[at, :]
            linp = jnp.sum(gop, axis=1, keepdims=True)
            for j in range(per_block):
                here = lane_id == b * per_block + j
                tissue = jnp.where(here, line[j * cap : (j + 1) * cap], tissue)
                cable = jnp.where(here, linp[j * cap : (j + 1) * cap], cable)
            return tissue, cable

        zero = jnp.zeros((cap, LANES), F32)
        tissue, cable = lax.fori_loop(0, slots // block, step, (zero, zero))
        qt[0:cap, :] = tissue
        qp[0:cap, :] = cable
        turned_t = jnp.transpose(qt[...])
        turned_p = jnp.transpose(qp[...])
        for d in range(D):
            send[k, d, 0:1, :] = turned_p[d : d + 1, :]
            send[k, d, 1:2, :] = turned_t[d : d + 1, :]
        over_partners(functools.partial(junction_copy, k), lambda c: c.start())
        recv[k, me] = send[k, me]

    def currents(k):
        over_partners(functools.partial(junction_copy, k), lambda c: c.wait_recv())
        for d in range(D):
            ta[d : d + 1, :] = recv[k, d, 0:1, :]
            tb[d : d + 1, :] = recv[k, d, 1:2, :]
        rate = time_step * gap_conductance
        into_t = rate * (jnp.transpose(ta[...])[:cap, :] - qt[0:cap, :])
        into_p = rate * (qp[0:cap, :] - jnp.transpose(tb[...])[:cap, :])
        for d in range(D):
            at = slice(d * cap, (d + 1) * cap)
            high, low = pieces(into_t[:, d : d + 1] * lm[at, :])
            ws[at, 0:cz] = high
            ws[at, cz : 2 * cz] = low
            high, low = pieces(into_p[:, d : d + 1] * lmp[at, :])
            wps[at, 0:N] = high
            wps[at, N : 2 * N] = low

    row_id = lax.broadcasted_iota(jnp.int32, (cy, 1), 0)
    z_id = lax.broadcasted_iota(jnp.int32, (1, cz), 1)

    def beside(k, i):
        c = vp[k, i + 1]
        side = hyr[k, pl.ds(i, 1), :]
        yp = jnp.where(row_id == cy - 1, side, pltpu.roll(c, cy - 1, 0))
        ym = jnp.where(row_id == 0, side, pltpu.roll(c, 1, 0))
        return c, (vp[k, i + 2], vp[k, i], yp, ym, pltpu.roll(c, cz - 1, 1), pltpu.roll(c, 1, 1))

    def weights(i):
        return (gxf[i + 1], gxf[i], gyp[i], gym[i], gzp[i], gzm[i])

    def face(a, b):
        return jnp.where(jnp.minimum(a, b) > 0.0, 0.5 * (a + b), 0.0)

    def faces(i, _):
        c = vp[4, i + 1]
        side = hyr[4, pl.ds(i, 1), :]
        below = jnp.where(gy > 0, side, 0.0)
        above = jnp.where(gy < grid_y - 1, side, 0.0)
        gxf[i] = face(vp[4, i], c)
        gyp[i] = face(c, jnp.where(row_id == cy - 1, above, pltpu.roll(c, cy - 1, 0)))
        gym[i] = face(c, jnp.where(row_id == 0, below, pltpu.roll(c, 1, 0)))
        gzp[i] = face(c, jnp.where(z_id == cz - 1, 0.0, pltpu.roll(c, cz - 1, 1)))
        gzm[i] = face(c, jnp.where(z_id == 0, 0.0, pltpu.roll(c, 1, 1)))
        return 0

    def cable(k, old, out):
        for c in cable_copies(k):
            c.wait_recv()
        if k == 0:
            for j in (1, 2):
                kid_copy(j).wait_recv()
        tail_rows = [tailr[k, 1], tailr[k, 0], tails[k]]
        head_rows = [heads[k], headr[k, 0], headr[k, 1]]
        kid_rows = [kids[...], kidr[0], kidr[1]]
        step = 64

        def part(b, _):
            at = pl.ds(pl.multiple_of(b * step, step), step)
            y = ys[k, at, :]
            p = pb[at, :]
            has = p[:, 0:1] >= 0.0
            p = jnp.where(p >= 0.0, p, -1e6)
            s = sb[at, :]
            tail = y[:, N - 1 : N]
            ids = (lax.broadcasted_iota(jnp.int32, (step, 1), 0) + b * step + me * S).astype(F32)
            up = jnp.zeros((step, LANES), F32)
            down = jnp.zeros((step, LANES), F32)
            for w in range(3):
                for c in range(S // LANES):
                    cut = slice(c * LANES, (c + 1) * LANES)
                    window = (lane_id + ((me + (w - 2)) * S + c * LANES)).astype(F32)
                    up = up + jnp.where(p == window, tail_rows[w][:, cut], 0.0)
                    sk = kid_rows[w][0:1, cut]
                    down = down + jnp.where(
                        kid_rows[w][1:2, cut] == ids, sk * (head_rows[w][:, cut] - tail), 0.0
                    )
            parent_tail = jnp.sum(up, axis=1, keepdims=True)
            inflow = jnp.sum(down, axis=1, keepdims=True)
            head = jnp.where(has, s[:, 0:1] * (parent_tail - y[:, 0:1]), 0.0)
            node = lax.broadcasted_iota(jnp.int32, (1, N), 1)
            step_up = jnp.where(node < N - 1, pltpu.roll(y, N - 1, 1) - y, 0.0)
            edge = s * step_up
            flux = edge - pltpu.roll(edge, 1, 1)
            flux = flux + jnp.where(node == 0, head, 0.0) + jnp.where(node == N - 1, inflow, 0.0)
            if old is None:
                ptb[k, at, :] = jnp.broadcast_to(parent_tail, (step, LANES))
                out[at, :] = y + time_step * (flux + ionic(y))
            else:
                u = ys[old, at, :]
                rise = jnp.where(node < N - 1, pltpu.roll(u, N - 1, 1) - u, 0.0)
                inner = jnp.sum(-step_up * rise, axis=1, keepdims=True)
                over = jnp.where(
                    has, (y[:, 0:1] - parent_tail) * (ptb[old, at, 0:1] - u[:, 0:1]), 0.0
                )
                pgb[at, :] = pgb[at, :] + time_step * (inner + over)
                out[at, :] = y + time_step * (flux + slope(u) * y)
            return 0

        lax.fori_loop(0, S // step, part, 0)

    group = 4 if cx % 4 == 0 else 1

    def spread(finish):
        def step(b, _):
            at = pl.ds(pl.multiple_of(b * (group * cy), group * cy), group * cy)
            add = dot(ott[at, :], ws[...])
            add = add[:, :cz] + add[:, cz:]
            for g in range(group):
                finish(b * group + g, add[g * cy : (g + 1) * cy])
            return 0

        lax.fori_loop(0, cx // group, step, 0)

    def spread_cable():
        add = dot(opt[...], wps[...])
        return add[:, :N] + add[:, N:]

    for k in range(2):
        gather(k)
        if k == 0:
            halo_wait(4)
            lax.fori_loop(0, cx, faces, 0)
            gxf[cx] = face(vp[4, cx], vp[4, cx + 1])
        halo_wait(k)

        def forward(i, _, k=k):
            c, others = beside(k, i)
            total = zero_plane
            for g, n in zip(weights(i), others):
                total = total + g * (n - c)
            new = c + time_step * (total + ionic(c))
            if k == 0:
                vp[1, i + 1] = new
            else:
                v2b[i] = new
            return 0

        lax.fori_loop(0, cx, forward, 0)
        out = ys.at[1] if k == 0 else y2b
        cable(k, None, out)
        currents(k)
        out[...] = out[...] - spread_cable()
        if k == 0:
            def finish(i, add):
                new = vp[1, i + 1] + add
                vp[1, i + 1] = new
                hys[1, pl.ds(i, 1), :] = edge_row(new)
                split_plane(i, new)
        else:
            loads[4].wait()
            loads[5].wait()
            ys[2] = loss_weight * (y2b[...] - (1.0 - ptarget[...].astype(F32) / target_span))

            def finish(i, add):
                new = v2b[i] + add
                v2b[i] = new
                goal = 1.0 - target[i].astype(F32) / target_span
                seed = jnp.where(vp[4, i + 1] > 0.0, loss_weight * (new - goal), 0.0)
                vp[2, i + 1] = seed
                hys[2, pl.ds(i, 1), :] = edge_row(seed)
                split_plane(i, seed)
        cable_start(k + 1)
        spread(finish)
        halo_start(k + 1)

    stores = [
        pltpu.make_async_copy(v2b, v2_o, loc_sem.at[6]),
        pltpu.make_async_copy(y2b, y2_o, loc_sem.at[7]),
    ]
    for c in stores:
        c.start()

    for k in (2, 3):
        old = 3 - k
        gather(k)
        halo_wait(k)

        def backward(i, _, k=k, old=old):
            c, others = beside(k, i)
            v, befores = beside(old, i)
            total = zero_plane
            grad = zero_plane
            for g, n, b in zip(weights(i), others, befores):
                d = n - c
                total = total + g * d
                grad = grad + jnp.where(g > 0.0, d * (v - b), 0.0)
            new = c + time_step * (total + slope(v) * c)
            grad = (0.5 * time_step) * grad
            if k == 2:
                vp[3, i + 1] = new
                gsb[i] = grad
            else:
                l0b[i] = new
                gsb[i] = gsb[i] + grad
            return 0

        lax.fori_loop(0, cx, backward, 0)
        out = ys.at[3] if k == 2 else mu0b
        cable(k, old, out)
        currents(k)
        out[...] = out[...] - spread_cable()
        if k == 2:
            cable_start(3)

            def finish(i, add):
                new = vp[3, i + 1] + add
                vp[3, i + 1] = new
                hys[3, pl.ds(i, 1), :] = edge_row(new)
                split_plane(i, new)
        else:
            stores.append(pltpu.make_async_copy(gsb, gs_o, loc_sem.at[8]))
            stores[-1].start()
            stores.append(pltpu.make_async_copy(mu0b, mu_o, loc_sem.at[9]))
            stores[-1].start()
            gp_o[...] = jnp.transpose(pgb[...])[0:1, :]

            def finish(i, add):
                l0b[i] = l0b[i] + add
        spread(finish)
        if k == 2:
            halo_start(3)

    stores.append(pltpu.make_async_copy(l0b, la_o, loc_sem.at[10]))
    stores[-1].start()
    over_partners(vox_copy, lambda c: c.wait_send())
    for j in (1, 2):
        kid_copy(j).wait_send()
    for k in range(5):
        halo_sent(k)
    for k in range(4):
        over_partners(functools.partial(junction_copy, k), lambda c: c.wait_send())
        for c in cable_copies(k):
            c.wait_send()
    for c in stores:
        c.wait()


def body(
    initial_voltage, conductivity, tissue_mask, target_step, initial_purkinje,
    purkinje_conductivity, segment_parent, purkinje_target, junction_voxel, junction_node,
):
    cx, cy, cz = initial_voltage.shape
    S, N = initial_purkinje.shape
    grid_x = lax.axis_size("gx")
    grid_y = lax.axis_size("gy")
    assert grid_y == 2 and N == LANES
    D = grid_x * grid_y
    per_device = junction_voxel.shape[0]
    cap = max(16, 2 * per_device // D)
    assert cap <= LANES and D <= LANES
    slots = D * cap
    rows = cx * cy

    plane = cy * grid_y * cz
    first = junction_voxel // plane
    rest = junction_voxel % plane
    second = rest // cz
    third = rest % cz
    owner = first // cx * grid_y + second // cy
    local_voxel = (first % cx * cy + second % cy) * cz + third
    local_node = junction_node % (S * N)
    ordinal = jnp.arange(per_device, dtype=jnp.int32)
    same = owner[:, None] == owner[None, :]
    earlier = ordinal[:, None] < ordinal[None, :]
    rank = jnp.sum((same & earlier).astype(jnp.int32), axis=0)
    slot = owner * LANES + rank
    match = jnp.arange(D * LANES, dtype=jnp.int32)[:, None] == slot[None, :]
    slot_voxel = jnp.sum(jnp.where(match, local_voxel[None, :] + 1, 0), axis=1) - 1
    slot_node = jnp.sum(jnp.where(match, local_node[None, :] + 1, 0), axis=1) - 1
    slot_voxel = slot_voxel.astype(F32).reshape(D, 1, LANES)
    slot_node = slot_node.astype(F32).reshape(D, 1, LANES)

    any_spec = pl.BlockSpec(memory_space=pl.ANY)
    vmem = pl.BlockSpec(memory_space=pltpu.VMEM)
    V = pltpu.VMEM
    dma = pltpu.SemaphoreType.DMA
    field = V((cx, cy, cz), F32)
    fibre = V((S, N), F32)
    scratch = [
        V((5, cx + 2, cy, cz), F32), V((5, cx, cz), F32), V((5, cx, cz), F32),
        V((cx, cy, cz), jnp.int32), V((cx, cy, cz), jnp.int32), V((cx + 1, cy, cz), F32),
        field, field, field, field, field, field, field,
        V((4, S, N), F32), fibre, fibre, V((S, N), jnp.int32), V((S, LANES), F32),
        V((S, LANES), F32), V((2, S, LANES), F32), V((S, LANES), F32),
        V((slots, rows), BF16), V((rows, slots), BF16), V((slots, cz), F32),
        V((rows, 2 * cz), BF16), V((slots, 2 * cz), BF16),
        V((slots, S), BF16), V((S, slots), BF16), V((slots, N), F32),
        V((S, 2 * N), BF16), V((slots, 2 * N), BF16),
        V((LANES, LANES), F32), V((LANES, LANES), F32), V((LANES, LANES), F32),
        V((LANES, LANES), F32), V((slots, LANES), F32), V((slots, LANES), F32),
        V((4, D, 2, LANES), F32), V((4, D, 2, LANES), F32), V((D, 1, LANES), F32),
        V((4, 1, S), F32), V((4, 1, S), F32), V((4, 2, 1, S), F32), V((4, 2, 1, S), F32),
        V((2, S), F32), V((2, 2, S), F32),
        dma((11,)), dma((4, D)), dma((4, D)), dma((D,)), dma((D,)),
        dma((5, 2)), dma((5, 2)), dma((5,)), dma((5,)), dma((4, 4)), dma((4, 4)),
        dma((2,)), dma((2,)),
    ]
    tissue = jax.ShapeDtypeStruct((cx, cy, cz), F32)
    cable = jax.ShapeDtypeStruct((S, N), F32)
    v2, y2, gs, gp, la, mu = pl.pallas_call(
        functools.partial(kernel, grid_x, grid_y, cap),
        name="monodomain",
        out_shape=(tissue, cable, tissue, jax.ShapeDtypeStruct((1, S), F32), tissue, cable),
        in_specs=[any_spec] * 5 + [vmem] * 2 + [any_spec] + [vmem] * 2,
        out_specs=(any_spec, any_spec, any_spec, vmem, any_spec, any_spec),
        scratch_shapes=scratch,
        compiler_params=pltpu.CompilerParams(
            collective_id=0, has_side_effects=True, vmem_limit_bytes=62 * 1024 * 1024
        ),
    )(
        initial_voltage, conductivity, tissue_mask, target_step, initial_purkinje,
        purkinje_conductivity.reshape(1, S), segment_parent.astype(F32).reshape(1, S),
        purkinje_target, slot_voxel, slot_node,
    )
    return v2, y2, gs, gp.reshape(S), la, mu


def solution(mesh):
    tissue = P(("groups", "gx"), "gy", None)
    cable = P(("groups", "gx", "gy"), None)
    line = P(("groups", "gx", "gy"))
    return jax.shard_map(
        body,
        mesh=mesh,
        in_specs=(tissue, tissue, tissue, tissue, cable, line, line, cable, line, line),
        out_specs=(tissue, cable, tissue, line, tissue, cable),
        check_vma=False,
    )
```

```python
import functools

import jax
import jax.numpy as jnp
from jax import lax
from jax.experimental import pallas as pl
from jax.experimental.pallas import tpu as pltpu
from jax.sharding import PartitionSpec as P

time_step = 0.05
gap_conductance = 4.0
ion_rate = 8.0
threshold = 0.15
loss_weight = 10.0
target_span = 8.0
LANES = 128
F32 = jnp.float32
BF16 = jnp.bfloat16


def ionic(values):
    return ion_rate * values * (values - threshold) * (1.0 - values)


def slope(values):
    return ion_rate * (-3.0 * values * values + 2.0 * (1.0 + threshold) * values - threshold)


def pieces(values):
    high = values.astype(BF16)
    return high, (values - high.astype(F32)).astype(BF16)


def dot(a, b):
    return lax.dot_general(a, b, (((1,), (0,)), ((), ())), preferred_element_type=F32)


def dot_t(a, b):
    return lax.dot_general(a, b, (((1,), (1,)), ((), ())), preferred_element_type=F32)


def stacked_pieces(values):
    high = values.astype(BF16)
    rest = values - high.astype(F32)
    middle = rest.astype(BF16)
    return jnp.concatenate([high, middle, (rest - middle.astype(F32)).astype(BF16)], axis=0)


def summed(values):
    n = values.shape[0] // 3
    return values[:n] + values[n : 2 * n] + values[2 * n :]


def bits(size):
    assert size & (size - 1) == 0
    return size.bit_length() - 1


def kernel(
    grid_x, grid_y, cap,
    v0_h, sigma_h, mask_h, target_h, y0_h, sigma_row, parent_int, ptarget_h, junction_voxel, junction_node,
    v2_o, y2_o, gs_o, gp_o, la_o, mu_o,
    vp, hys, hyr, tmp_mask, target, gxf, gym, gyp, gzm, gzp, v2b, l0b, gsb,
    ys, y2b, mu0b, ptarget, sb, ends, pgb, pgr, ptr, plt_s, phm, kb, khm, kid_sigma, kid_total,
    ot, ott, lm, lmb, xs, ws, op, opt, lmp, lmpb, yss, wps, slot_voxel,
    qt, qp, ta, tb, colb, colp, send, recv, voxr,
    tails, heads, tailr, headr, kids, kidr,
    loc_sem, js, jr, vs, vr, xs_s, xs_r, ysm_s, ysm_r, cs_s, cs_r, ks_s, ks_r,
):
    D = grid_x * grid_y
    cx, cy, cz = v2b.shape
    S, N = y2b.shape
    slots = D * cap
    rows = cx * cy
    gx = lax.axis_index("gx")
    gy = lax.axis_index("gy")
    me = gx * grid_y + gy

    def dev(flat):
        return {"gx": lax.div(flat, grid_y), "gy": lax.rem(flat, grid_y)}

    def rc(src, dst, s, r, where):
        return pltpu.make_async_remote_copy(
            src_ref=src, dst_ref=dst, send_sem=s, recv_sem=r,
            device_id=where, device_id_type=pl.DeviceIdType.MESH,
        )

    loads = [
        pltpu.make_async_copy(v0_h, vp.at[0, pl.ds(1, cx)], loc_sem.at[0]),
        pltpu.make_async_copy(sigma_h, gsb, loc_sem.at[1]),
        pltpu.make_async_copy(mask_h, tmp_mask, loc_sem.at[2]),
        pltpu.make_async_copy(y0_h, ys.at[0], loc_sem.at[3]),
        pltpu.make_async_copy(target_h, target, loc_sem.at[4]),
        pltpu.make_async_copy(ptarget_h, ptarget, loc_sem.at[5]),
    ]
    for c in loads:
        c.start()

    barrier = pltpu.get_barrier_semaphore()

    def greet(o, _):
        pl.semaphore_signal(
            barrier, inc=1, device_id=dev(lax.rem(me + o, D)), device_id_type=pl.DeviceIdType.MESH
        )
        return 0

    lax.fori_loop(1, D, greet, 0)
    kids[0:1, :] = sigma_row[...]
    parent_row = parent_int[...].astype(F32)
    kids[1:2, :] = parent_row

    J = junction_voxel.shape[1]
    voxel = junction_voxel[...]
    y_full = cy * grid_y
    z_at = voxel & (cz - 1)
    y_at = lax.shift_right_logical(voxel, bits(cz)) & (y_full - 1)
    x_at = lax.shift_right_logical(voxel, bits(cz) + bits(y_full))
    owner = lax.shift_right_logical(x_at, bits(cx)) * grid_y + lax.shift_right_logical(y_at, bits(cy))
    local_voxel = ((x_at & (cx - 1)) * cy + (y_at & (cy - 1))) * cz + z_at
    local_node = junction_node[...] & (S * N - 1)
    mine = jnp.where(lax.broadcasted_iota(jnp.int32, (D, J), 0) == owner, 1.0, 0.0)
    ahead = jnp.where(
        lax.broadcasted_iota(jnp.int32, (J, J), 0) < lax.broadcasted_iota(jnp.int32, (J, J), 1), 1.0, 0.0
    ).astype(BF16)
    rank = jnp.sum(mine * dot(mine.astype(BF16), ahead), axis=0, keepdims=True)
    rank_t = jnp.where(
        lax.broadcasted_iota(jnp.int32, (LANES, J), 0).astype(F32) == rank, 1.0, 0.0
    ).astype(BF16)
    parts = [mine]
    for value in (local_voxel, local_node):
        for shift in (0, 8, 16):
            digit = (lax.shift_right_logical(value, shift) & 255).astype(F32)
            parts.append(mine * digit)
    table = dot_t(jnp.concatenate(parts, axis=0).astype(BF16), rank_t)

    def number(first):
        a, b, c = (table[(first + n) * D : (first + n + 1) * D] for n in range(3))
        return a + 256.0 * b + 65536.0 * c + table[:D] - 1.0

    slot_number = number(1)
    slot_node = number(4)
    for d in range(D):
        slot_voxel[d] = slot_number[d : d + 1, :]
    pl.semaphore_wait(barrier, D - 1)

    def vox_copy(o):
        to = lax.rem(me + o, D)
        return rc(slot_voxel.at[to], voxr.at[me], vs.at[o], vr.at[o], dev(to))

    def junction_copy(k, o):
        to = lax.rem(me + o, D)
        return rc(send.at[k, to], recv.at[k, me], js.at[k, o], jr.at[k, o], dev(to))

    def over_partners(make, act):
        def step(o, _):
            act(make(o))
            return 0

        lax.fori_loop(1, D, step, 0)

    def kid_copy(j):
        return rc(kids, kidr.at[j - 1], ks_s.at[j - 1], ks_r.at[j - 1], dev(lax.rem(me + D - j, D)))

    def cable_copies(k):
        out = []
        for j in (1, 2):
            out.append(rc(tails.at[k], tailr.at[k, j - 1], cs_s.at[k, j - 1], cs_r.at[k, j - 1],
                          dev(lax.rem(me + j, D))))
            out.append(rc(heads.at[k], headr.at[k, j - 1], cs_s.at[k, j + 1], cs_r.at[k, j + 1],
                          dev(lax.rem(me + D - j, D))))
        return out

    def up_copy(k):
        return rc(vp.at[k, cx], vp.at[k, 0], xs_s.at[k, 0], xs_r.at[k, 0],
                  {"gx": lax.rem(gx + 1, grid_x), "gy": gy})

    def down_copy(k):
        return rc(vp.at[k, 1], vp.at[k, cx + 1], xs_s.at[k, 1], xs_r.at[k, 1],
                  {"gx": lax.rem(gx + grid_x - 1, grid_x), "gy": gy})

    def side_copy(k):
        return rc(hys.at[k], hyr.at[k], ysm_s.at[k], ysm_r.at[k], {"gx": gx, "gy": 1 - gy})

    def halo_start(k):
        @pl.when(gx < grid_x - 1)
        def _():
            up_copy(k).start()

        @pl.when(gx > 0)
        def _():
            down_copy(k).start()

        side_copy(k).start()

    def halo_wait(k):
        @pl.when(gx > 0)
        def _():
            up_copy(k).wait_recv()

        @pl.when(gx < grid_x - 1)
        def _():
            down_copy(k).wait_recv()

        side_copy(k).wait_recv()

    def halo_sent(k):
        @pl.when(gx < grid_x - 1)
        def _():
            up_copy(k).wait_send()

        @pl.when(gx > 0)
        def _():
            down_copy(k).wait_send()

        side_copy(k).wait_send()

    over_partners(vox_copy, lambda c: c.start())
    for j in (1, 2):
        kid_copy(j).start()
    voxr[me] = slot_voxel[me]

    zero_plane = jnp.zeros((cy, cz), F32)

    @pl.when(gx == 0)
    def _():
        for k in range(5):
            vp[k, 0] = zero_plane

    @pl.when(gx == grid_x - 1)
    def _():
        for k in range(5):
            vp[k, cx + 1] = zero_plane

    def split_plane(i, c):
        high, low = pieces(c)
        at = pl.ds(pl.multiple_of(i * cy, cy), cy)
        xs[at, 0:cz] = high
        xs[at, cz : 2 * cz] = low

    def edge_row(c):
        return jnp.where(gy == 0, c[cy - 1 : cy, :], c[0:1, :])

    for n in range(4):
        loads[n].wait()

    def prepare(i, _):
        masked = gsb[i] * tmp_mask[i].astype(F32)
        vp[4, i + 1] = masked
        hys[4, pl.ds(i, 1), :] = edge_row(masked)
        c = vp[0, i + 1]
        hys[0, pl.ds(i, 1), :] = edge_row(c)
        split_plane(i, c)
        return 0

    lax.fori_loop(0, cx, prepare, 0)
    halo_start(0)
    halo_start(4)

    def cable_start(k):
        y = ys[k]
        turned = jnp.transpose(y)
        tails[k] = turned[N - 1 : N, :]
        heads[k] = turned[0:1, :]
        for c in cable_copies(k):
            c.start()
        high, low = pieces(y)
        yss[:, 0:N] = high
        yss[:, N : 2 * N] = low

    cable_start(0)
    chunks = S // LANES
    whose = lax.broadcasted_iota(jnp.int32, (LANES, 1), 0).astype(F32)
    has_parent = parent_row >= 0.0
    window = jnp.where(has_parent, parent_row - ((me - 2) * S).astype(F32), -1.0)
    window_high = jnp.floor(window * (1.0 / LANES))
    plt_s[...] = jnp.where(whose == window - window_high * LANES, 1.0, 0.0).astype(BF16)
    phm[...] = jnp.where(
        lax.broadcasted_iota(jnp.int32, phm.shape, 0).astype(F32) == window_high, 1.0, 0.0
    )
    sb[...] = jnp.transpose(jnp.broadcast_to(sigma_row[...], (LANES, S)))
    pgb[...] = jnp.zeros_like(pgb)
    pgr[...] = jnp.zeros_like(pgr)

    def build(width, depth, onehot, onehot_t, lane_mask, lane_mask_b, column):
        index = jnp.transpose(ta[...])[:cap, :]
        row = jnp.floor(index * (1.0 / width))
        lane = index - row * width
        lane_of = lax.broadcasted_iota(jnp.int32, (1, width), 1).astype(F32)
        row_of = lax.broadcasted_iota(jnp.int32, (1, depth), 1).astype(F32)
        for d in range(D):
            at = slice(d * cap, (d + 1) * cap)
            r = row[:, d : d + 1]
            onehot[at, :] = jnp.where(r == row_of, 1.0, 0.0).astype(BF16)
            hit = jnp.where(lane[:, d : d + 1] == lane_of, 1.0, 0.0)
            lane_mask[at, :] = hit
            lane_mask_b[at, :] = hit.astype(BF16)
            column[at, :] = jnp.broadcast_to(r, (cap, LANES))
        row_line = jnp.transpose(column[...])[0:1, :]
        step = 64

        def fill(b, _):
            ids = (lax.broadcasted_iota(jnp.int32, (step, 1), 0) + b * step).astype(F32)
            onehot_t[pl.ds(pl.multiple_of(b * step, step), step), :] = jnp.where(
                ids == row_line, 1.0, 0.0
            ).astype(BF16)
            return 0

        lax.fori_loop(0, depth // step, fill, 0)

    ta[...] = jnp.zeros_like(ta)
    ta[0:D, :] = slot_node
    build(N, S, op, opt, lmp, lmpb, colp)
    for j in (1, 2):
        kid_copy(j).wait_recv()
    kid_rows = [kids[...], kidr[0], kidr[1]]
    for w in range(3):
        cut = slice(w * S, (w + 1) * S)
        near = kid_rows[w][1:2, :] - (me * S).astype(F32)
        near_high = jnp.floor(near * (1.0 / LANES))
        hit = jnp.where(whose == near - near_high * LANES, 1.0, 0.0)
        kb[cut, :] = jnp.transpose(hit).astype(BF16)
        ids = lax.broadcasted_iota(jnp.int32, (khm.shape[0], 1), 0)
        ids = jnp.where(ids < chunks, ids, -1000000).astype(F32)
        khm[:, cut] = jnp.where(ids == near_high, 1.0, 0.0)
        kid_sigma[:, cut] = kid_rows[w][0:1, :]
    kid_total[...] = summed(dot(stacked_pieces(khm[...] * kid_sigma[...]), kb[...]))
    over_partners(vox_copy, lambda c: c.wait_recv())
    for d in range(D):
        ta[d : d + 1, :] = voxr[d]
    build(cz, rows, ot, ott, lm, lmb, colb)

    lane_id = lax.broadcasted_iota(jnp.int32, (1, LANES), 1)
    block = min(slots, 512)
    per_block = block // cap
    qt[...] = jnp.zeros_like(qt)
    qp[...] = jnp.zeros_like(qp)

    def gather(k):
        def step(b, carry):
            tissue, cable = carry
            at = pl.ds(pl.multiple_of(b * block, block), block)
            got = dot(ot[at, :], xs[...])
            got = (got[:, :cz] + got[:, cz:]) * lm[at, :]
            line = jnp.sum(got, axis=1, keepdims=True)
            gop = dot(op[at, :], yss[...])
            gop = (gop[:, :N] + gop[:, N:]) * lmp[at, :]
            linp = jnp.sum(gop, axis=1, keepdims=True)
            for j in range(per_block):
                here = lane_id == b * per_block + j
                tissue = jnp.where(here, line[j * cap : (j + 1) * cap], tissue)
                cable = jnp.where(here, linp[j * cap : (j + 1) * cap], cable)
            return tissue, cable

        zero = jnp.zeros((cap, LANES), F32)
        tissue, cable = lax.fori_loop(0, slots // block, step, (zero, zero))
        qt[0:cap, :] = tissue
        qp[0:cap, :] = cable
        turned_t = jnp.transpose(qt[...])
        turned_p = jnp.transpose(qp[...])
        for d in range(D):
            send[k, d, 0:1, :] = turned_p[d : d + 1, :]
            send[k, d, 1:2, :] = turned_t[d : d + 1, :]
        over_partners(functools.partial(junction_copy, k), lambda c: c.start())
        recv[k, me] = send[k, me]

    def currents(k):
        over_partners(functools.partial(junction_copy, k), lambda c: c.wait_recv())
        for d in range(D):
            ta[d : d + 1, :] = recv[k, d, 0:1, :]
            tb[d : d + 1, :] = recv[k, d, 1:2, :]
        rate = time_step * gap_conductance
        into_t = rate * (jnp.transpose(ta[...])[:cap, :] - qt[0:cap, :])
        into_p = rate * (qp[0:cap, :] - jnp.transpose(tb[...])[:cap, :])
        high_t, low_t = pieces(into_t)
        high_p, low_p = pieces(into_p)
        for d in range(D):
            at = slice(d * cap, (d + 1) * cap)
            ws[at, 0:cz] = high_t[:, d : d + 1] * lmb[at, :]
            ws[at, cz : 2 * cz] = low_t[:, d : d + 1] * lmb[at, :]
            wps[at, 0:N] = high_p[:, d : d + 1] * lmpb[at, :]
            wps[at, N : 2 * N] = low_p[:, d : d + 1] * lmpb[at, :]

    row_id = lax.broadcasted_iota(jnp.int32, (cy, 1), 0)
    z_id = lax.broadcasted_iota(jnp.int32, (1, cz), 1)

    def beside(k, i):
        c = vp[k, i + 1]
        side = hyr[k, pl.ds(i, 1), :]
        yp = jnp.where(row_id == cy - 1, side, pltpu.roll(c, cy - 1, 0))
        ym = jnp.where(row_id == 0, side, pltpu.roll(c, 1, 0))
        return c, (vp[k, i + 2], vp[k, i], yp, ym, pltpu.roll(c, cz - 1, 1), pltpu.roll(c, 1, 1))

    def weights(i):
        return (gxf[i + 1], gxf[i], gyp[i], gym[i], gzp[i], gzm[i])

    def face(a, b):
        return jnp.where(jnp.minimum(a, b) > 0.0, 0.5 * (a + b), 0.0)

    def faces(i, _):
        c = vp[4, i + 1]
        side = hyr[4, pl.ds(i, 1), :]
        below = jnp.where(gy > 0, side, 0.0)
        above = jnp.where(gy < grid_y - 1, side, 0.0)
        gxf[i] = face(vp[4, i], c)
        gyp[i] = face(c, jnp.where(row_id == cy - 1, above, pltpu.roll(c, cy - 1, 0)))
        gym[i] = face(c, jnp.where(row_id == 0, below, pltpu.roll(c, 1, 0)))
        gzp[i] = face(c, jnp.where(z_id == cz - 1, 0.0, pltpu.roll(c, cz - 1, 1)))
        gzm[i] = face(c, jnp.where(z_id == 0, 0.0, pltpu.roll(c, 1, 1)))
        return 0

    def cable(k, old, out):
        for c in cable_copies(k):
            c.wait_recv()
        tail_rows = [tailr[k, 1], tailr[k, 0], tails[k]]
        own_heads = heads[k]
        lines = [t[:, c * LANES : (c + 1) * LANES] for t in tail_rows for c in range(chunks)]
        pad = phm.shape[0] - len(lines)
        if pad:
            lines.append(jnp.zeros((pad, LANES), F32))
        found = summed(dot(stacked_pieces(jnp.concatenate(lines, axis=0)), plt_s[...]))
        parent_tail = jnp.sum(phm[...] * found, axis=0, keepdims=True)
        kid_heads = jnp.concatenate([own_heads, headr[k, 0], headr[k, 1]], axis=1)
        sums = summed(dot(stacked_pieces(khm[...] * (kid_sigma[...] * kid_heads)), kb[...]))
        inflow = jnp.concatenate(
            [
                sums[c : c + 1] - lines[2 * chunks + c] * kid_total[c : c + 1, :]
                for c in range(chunks)
            ],
            axis=1,
        )
        head = jnp.where(has_parent, sigma_row[...] * (parent_tail - own_heads), 0.0)
        place = lax.broadcasted_iota(jnp.int32, (N, 1), 0)
        ends[...] = jnp.transpose(
            jnp.where(place == 0, head, 0.0) + jnp.where(place == N - 1, inflow, 0.0)
        )
        if old is None:
            ptr[k] = parent_tail
        else:
            over = (own_heads - parent_tail) * (ptr[old] - heads[old])
            pgr[...] = pgr[...] + time_step * jnp.where(has_parent, over, 0.0)
        step = 64
        node = lax.broadcasted_iota(jnp.int32, (1, N), 1)

        def part(b, _):
            at = pl.ds(pl.multiple_of(b * step, step), step)
            y = ys[k, at, :]
            step_up = jnp.where(node < N - 1, pltpu.roll(y, N - 1, 1) - y, 0.0)
            edge = sb[at, :] * step_up
            flux = edge - pltpu.roll(edge, 1, 1) + ends[at, :]
            if old is None:
                out[at, :] = y + time_step * (flux + ionic(y))
            else:
                u = ys[old, at, :]
                rise = jnp.where(node < N - 1, pltpu.roll(u, N - 1, 1) - u, 0.0)
                pgb[at, :] = pgb[at, :] - time_step * (step_up * rise)
                out[at, :] = y + time_step * (flux + slope(u) * y)
            return 0

        lax.fori_loop(0, S // step, part, 0)

    group = 4 if cx % 4 == 0 else 1

    def spread(finish):
        def step(b, _):
            at = pl.ds(pl.multiple_of(b * (group * cy), group * cy), group * cy)
            add = dot(ott[at, :], ws[...])
            add = add[:, :cz] + add[:, cz:]
            for g in range(group):
                finish(b * group + g, add[g * cy : (g + 1) * cy])
            return 0

        lax.fori_loop(0, cx // group, step, 0)

    def spread_cable():
        add = dot(opt[...], wps[...])
        return add[:, :N] + add[:, N:]

    for k in range(2):
        gather(k)
        if k == 0:
            halo_wait(4)
            lax.fori_loop(0, cx, faces, 0)
            gxf[cx] = face(vp[4, cx], vp[4, cx + 1])
        halo_wait(k)

        def forward(i, _, k=k):
            c, others = beside(k, i)
            total = zero_plane
            for g, n in zip(weights(i), others):
                total = total + g * (n - c)
            new = c + time_step * (total + ionic(c))
            if k == 0:
                vp[1, i + 1] = new
            else:
                v2b[i] = new
            return 0

        lax.fori_loop(0, cx, forward, 0)
        out = ys.at[1] if k == 0 else y2b
        cable(k, None, out)
        currents(k)
        out[...] = out[...] - spread_cable()
        if k == 0:
            def finish(i, add):
                new = vp[1, i + 1] + add
                vp[1, i + 1] = new
                hys[1, pl.ds(i, 1), :] = edge_row(new)
                split_plane(i, new)
        else:
            loads[4].wait()
            loads[5].wait()
            ys[2] = loss_weight * (y2b[...] - (1.0 - ptarget[...].astype(F32) / target_span))

            def finish(i, add):
                new = v2b[i] + add
                v2b[i] = new
                goal = 1.0 - target[i].astype(F32) / target_span
                seed = jnp.where(vp[4, i + 1] > 0.0, loss_weight * (new - goal), 0.0)
                vp[2, i + 1] = seed
                hys[2, pl.ds(i, 1), :] = edge_row(seed)
                split_plane(i, seed)
        cable_start(k + 1)
        spread(finish)
        halo_start(k + 1)

    stores = [
        pltpu.make_async_copy(v2b, v2_o, loc_sem.at[6]),
        pltpu.make_async_copy(y2b, y2_o, loc_sem.at[7]),
    ]
    for c in stores:
        c.start()

    for k in (2, 3):
        old = 3 - k
        gather(k)
        halo_wait(k)

        def backward(i, _, k=k, old=old):
            c, others = beside(k, i)
            v, befores = beside(old, i)
            total = zero_plane
            grad = zero_plane
            for g, n, b in zip(weights(i), others, befores):
                d = n - c
                total = total + g * d
                grad = grad + jnp.where(g > 0.0, d * (v - b), 0.0)
            new = c + time_step * (total + slope(v) * c)
            grad = (0.5 * time_step) * grad
            if k == 2:
                vp[3, i + 1] = new
                gsb[i] = grad
            else:
                l0b[i] = new
                gsb[i] = gsb[i] + grad
            return 0

        lax.fori_loop(0, cx, backward, 0)
        out = ys.at[3] if k == 2 else mu0b
        cable(k, old, out)
        currents(k)
        out[...] = out[...] - spread_cable()
        if k == 2:
            cable_start(3)

            def finish(i, add):
                new = vp[3, i + 1] + add
                vp[3, i + 1] = new
                hys[3, pl.ds(i, 1), :] = edge_row(new)
                split_plane(i, new)
        else:
            stores.append(pltpu.make_async_copy(gsb, gs_o, loc_sem.at[8]))
            stores[-1].start()
            stores.append(pltpu.make_async_copy(mu0b, mu_o, loc_sem.at[9]))
            stores[-1].start()
            gp_o[...] = pgr[...] + jnp.sum(jnp.transpose(pgb[...]), axis=0, keepdims=True)

            def finish(i, add):
                l0b[i] = l0b[i] + add
        spread(finish)
        if k == 2:
            halo_start(3)

    stores.append(pltpu.make_async_copy(l0b, la_o, loc_sem.at[10]))
    stores[-1].start()
    over_partners(vox_copy, lambda c: c.wait_send())
    for j in (1, 2):
        kid_copy(j).wait_send()
    for k in range(5):
        halo_sent(k)
    for k in range(4):
        over_partners(functools.partial(junction_copy, k), lambda c: c.wait_send())
        for c in cable_copies(k):
            c.wait_send()
    for c in stores:
        c.wait()


def body(
    initial_voltage, conductivity, tissue_mask, target_step, initial_purkinje,
    purkinje_conductivity, segment_parent, purkinje_target, junction_voxel, junction_node,
):
    cx, cy, cz = initial_voltage.shape
    S, N = initial_purkinje.shape
    grid_x = lax.axis_size("gx")
    grid_y = lax.axis_size("gy")
    assert grid_y == 2 and N == LANES
    D = grid_x * grid_y
    per_device = junction_voxel.shape[0]
    cap = max(16, 2 * per_device // D)
    assert cap <= LANES and D <= LANES
    slots = D * cap
    rows = cx * cy

    chunks = S // LANES
    window_rows = -(-3 * chunks // 16) * 16
    kid_rows = -(-chunks // 16) * 16

    any_spec = pl.BlockSpec(memory_space=pl.ANY)
    vmem = pl.BlockSpec(memory_space=pltpu.VMEM)
    hbm = pl.BlockSpec(memory_space=pltpu.HBM)
    V = pltpu.VMEM
    dma = pltpu.SemaphoreType.DMA
    field = V((cx, cy, cz), F32)
    fibre = V((S, N), F32)
    scratch = [
        V((5, cx + 2, cy, cz), F32), V((5, cx, cz), F32), V((5, cx, cz), F32),
        V((cx, cy, cz), jnp.int32), V((cx, cy, cz), jnp.int32), V((cx + 1, cy, cz), F32),
        field, field, field, field, field, field, field,
        V((4, S, N), F32), fibre, fibre, V((S, N), jnp.int32), V((S, LANES), F32),
        fibre, fibre, V((1, S), F32), V((2, 1, S), F32), V((LANES, S), BF16), V((window_rows, S), F32),
        V((3 * S, LANES), BF16), V((kid_rows, 3 * S), F32), V((1, 3 * S), F32), V((kid_rows, LANES), F32),
        V((slots, rows), BF16), V((rows, slots), BF16), V((slots, cz), F32), V((slots, cz), BF16),
        V((rows, 2 * cz), BF16), V((slots, 2 * cz), BF16),
        V((slots, S), BF16), V((S, slots), BF16), V((slots, N), F32), V((slots, N), BF16),
        V((S, 2 * N), BF16), V((slots, 2 * N), BF16), V((D, 1, LANES), F32),
        V((LANES, LANES), F32), V((LANES, LANES), F32), V((LANES, LANES), F32),
        V((LANES, LANES), F32), V((slots, LANES), F32), V((slots, LANES), F32),
        V((4, D, 2, LANES), F32), V((4, D, 2, LANES), F32), V((D, 1, LANES), F32),
        V((4, 1, S), F32), V((4, 1, S), F32), V((4, 2, 1, S), F32), V((4, 2, 1, S), F32),
        V((2, S), F32), V((2, 2, S), F32),
        dma((11,)), dma((4, D)), dma((4, D)), dma((D,)), dma((D,)),
        dma((5, 2)), dma((5, 2)), dma((5,)), dma((5,)), dma((4, 4)), dma((4, 4)),
        dma((2,)), dma((2,)),
    ]
    tissue = jax.ShapeDtypeStruct((cx, cy, cz), F32)
    cable = jax.ShapeDtypeStruct((S, N), F32)
    v2, y2, gs, gp, la, mu = pl.pallas_call(
        functools.partial(kernel, grid_x, grid_y, cap),
        name="monodomain",
        out_shape=(tissue, cable, tissue, jax.ShapeDtypeStruct((1, S), F32), tissue, cable),
        in_specs=[hbm] * 5 + [vmem] * 2 + [hbm] + [vmem] * 2,
        out_specs=(any_spec, any_spec, any_spec, vmem, any_spec, any_spec),
        scratch_shapes=scratch,
        compiler_params=pltpu.CompilerParams(
            collective_id=0, has_side_effects=True, vmem_limit_bytes=36 * 1024 * 1024
        ),
    )(
        initial_voltage, conductivity, tissue_mask, target_step, initial_purkinje,
        purkinje_conductivity.reshape(1, S), segment_parent.reshape(1, S),
        purkinje_target, junction_voxel.reshape(1, per_device), junction_node.reshape(1, per_device),
    )
    return v2, y2, gs, gp.reshape(S), la, mu


def solution(mesh):
    tissue = P(("groups", "gx"), "gy", None)
    cable = P(("groups", "gx", "gy"), None)
    line = P(("groups", "gx", "gy"))
    return jax.shard_map(
        body,
        mesh=mesh,
        in_specs=(tissue, tissue, tissue, tissue, cable, line, line, cable, line, line),
        out_specs=(tissue, cable, tissue, line, tissue, cable),
        check_vma=False,
    )
```

```python
import functools

import jax
import jax.numpy as jnp
from jax import lax
from jax.experimental import pallas as pl
from jax.experimental.pallas import tpu as pltpu
from jax.sharding import PartitionSpec as P

time_step = 0.05
gap_conductance = 4.0
ion_rate = 8.0
threshold = 0.15
loss_weight = 10.0
target_span = 8.0
LANES = 128
F32 = jnp.float32
BF16 = jnp.bfloat16


def ionic(values):
    return ion_rate * values * (values - threshold) * (1.0 - values)


def slope(values):
    return ion_rate * (-3.0 * values * values + 2.0 * (1.0 + threshold) * values - threshold)


def pieces(values):
    high = values.astype(BF16)
    return high, (values - high.astype(F32)).astype(BF16)


def dot(a, b):
    return lax.dot_general(a, b, (((1,), (0,)), ((), ())), preferred_element_type=F32)


def dot_t(a, b):
    return lax.dot_general(a, b, (((1,), (1,)), ((), ())), preferred_element_type=F32)


def stacked_pieces(values):
    high = values.astype(BF16)
    rest = values - high.astype(F32)
    middle = rest.astype(BF16)
    return jnp.concatenate([high, middle, (rest - middle.astype(F32)).astype(BF16)], axis=0)


def summed(values):
    n = values.shape[0] // 3
    return values[:n] + values[n : 2 * n] + values[2 * n :]


def bits(size):
    assert size & (size - 1) == 0
    return size.bit_length() - 1


def kernel(
    grid_x, grid_y, cap,
    v0_h, sigma_h, mask_h, target_h, y0_h, sigma_row, parent_int, ptarget_h, junction_voxel, junction_node,
    v2_o, y2_o, gs_o, gp_o, la_o, mu_o,
    vp, hys, hyr, tmp_mask, target, gxf, gym, gyp, gzm, gzp, v2b, l0b, gsb,
    ys, y2b, mu0b, ptarget, sb, ends, pgb, pgr, ptr, plt_s, phm, kb, khm, kid_sigma, kid_total,
    ot, ott, lm, lmb, xs, ws, op, opt, lmp, lmpb, yss, wps, slot_voxel,
    qt, qp, ta, tb, colb, colp, send, recv, voxr,
    tails, heads, tailr, headr, kids, kidr,
    loc_sem, js, jr, vs, vr, xs_s, xs_r, ysm_s, ysm_r, cs_s, cs_r, ks_s, ks_r,
):
    D = grid_x * grid_y
    cx, cy, cz = v2b.shape
    S, N = y2b.shape
    slots = D * cap
    rows = cx * cy
    gx = lax.axis_index("gx")
    gy = lax.axis_index("gy")
    me = gx * grid_y + gy

    def dev(flat):
        return {"gx": lax.div(flat, grid_y), "gy": lax.rem(flat, grid_y)}

    def rc(src, dst, s, r, where):
        return pltpu.make_async_remote_copy(
            src_ref=src, dst_ref=dst, send_sem=s, recv_sem=r,
            device_id=where, device_id_type=pl.DeviceIdType.MESH,
        )

    loads = [
        pltpu.make_async_copy(v0_h, vp.at[0, pl.ds(1, cx)], loc_sem.at[0]),
        pltpu.make_async_copy(sigma_h, gsb, loc_sem.at[1]),
        pltpu.make_async_copy(mask_h, tmp_mask, loc_sem.at[2]),
        pltpu.make_async_copy(y0_h, ys.at[0], loc_sem.at[3]),
        pltpu.make_async_copy(target_h, target, loc_sem.at[4]),
        pltpu.make_async_copy(ptarget_h, ptarget, loc_sem.at[5]),
    ]
    for c in loads:
        c.start()

    barrier = pltpu.get_barrier_semaphore()

    def greet(o, _):
        pl.semaphore_signal(
            barrier, inc=1, device_id=dev(lax.rem(me + o, D)), device_id_type=pl.DeviceIdType.MESH
        )
        return 0

    lax.fori_loop(1, D, greet, 0)
    kids[0:1, :] = sigma_row[...]
    parent_row = parent_int[...].astype(F32)
    kids[1:2, :] = parent_row

    J = junction_voxel.shape[1]
    voxel = junction_voxel[...]
    y_full = cy * grid_y
    z_at = voxel & (cz - 1)
    y_at = lax.shift_right_logical(voxel, bits(cz)) & (y_full - 1)
    x_at = lax.shift_right_logical(voxel, bits(cz) + bits(y_full))
    owner = lax.shift_right_logical(x_at, bits(cx)) * grid_y + lax.shift_right_logical(y_at, bits(cy))
    local_voxel = ((x_at & (cx - 1)) * cy + (y_at & (cy - 1))) * cz + z_at
    local_node = junction_node[...] & (S * N - 1)
    mine = jnp.where(lax.broadcasted_iota(jnp.int32, (D, J), 0) == owner, 1.0, 0.0)
    ahead = jnp.where(
        lax.broadcasted_iota(jnp.int32, (J, J), 0) < lax.broadcasted_iota(jnp.int32, (J, J), 1), 1.0, 0.0
    ).astype(BF16)
    rank = jnp.sum(mine * dot(mine.astype(BF16), ahead), axis=0, keepdims=True)
    rank_t = jnp.where(
        lax.broadcasted_iota(jnp.int32, (LANES, J), 0).astype(F32) == rank, 1.0, 0.0
    ).astype(BF16)
    parts = [mine]
    for value in (local_voxel, local_node):
        for shift in (0, 8, 16):
            digit = (lax.shift_right_logical(value, shift) & 255).astype(F32)
            parts.append(mine * digit)
    table = dot_t(jnp.concatenate(parts, axis=0).astype(BF16), rank_t)

    def number(first):
        a, b, c = (table[(first + n) * D : (first + n + 1) * D] for n in range(3))
        return a + 256.0 * b + 65536.0 * c + table[:D] - 1.0

    slot_number = number(1)
    slot_node = number(4)
    for d in range(D):
        slot_voxel[d] = slot_number[d : d + 1, :]
    pl.semaphore_wait(barrier, D - 1)

    def vox_copy(o):
        to = lax.rem(me + o, D)
        return rc(slot_voxel.at[to], voxr.at[me], vs.at[o], vr.at[o], dev(to))

    def junction_copy(k, o):
        to = lax.rem(me + o, D)
        return rc(send.at[k, to], recv.at[k, me], js.at[k, o], jr.at[k, o], dev(to))

    def over_partners(make, act):
        def step(o, _):
            act(make(o))
            return 0

        lax.fori_loop(1, D, step, 0)

    def kid_copy(j):
        return rc(kids, kidr.at[j - 1], ks_s.at[j - 1], ks_r.at[j - 1], dev(lax.rem(me + D - j, D)))

    def cable_copies(k):
        out = []
        for j in (1, 2):
            out.append(rc(tails.at[k], tailr.at[k, j - 1], cs_s.at[k, j - 1], cs_r.at[k, j - 1],
                          dev(lax.rem(me + j, D))))
            out.append(rc(heads.at[k], headr.at[k, j - 1], cs_s.at[k, j + 1], cs_r.at[k, j + 1],
                          dev(lax.rem(me + D - j, D))))
        return out

    def up_copy(k):
        return rc(vp.at[k, cx], vp.at[k, 0], xs_s.at[k, 0], xs_r.at[k, 0],
                  {"gx": lax.rem(gx + 1, grid_x), "gy": gy})

    def down_copy(k):
        return rc(vp.at[k, 1], vp.at[k, cx + 1], xs_s.at[k, 1], xs_r.at[k, 1],
                  {"gx": lax.rem(gx + grid_x - 1, grid_x), "gy": gy})

    def side_copy(k):
        return rc(hys.at[k], hyr.at[k], ysm_s.at[k], ysm_r.at[k], {"gx": gx, "gy": 1 - gy})

    def planes_start(k):
        @pl.when(gx < grid_x - 1)
        def _():
            up_copy(k).start()

        @pl.when(gx > 0)
        def _():
            down_copy(k).start()

    def halo_start(k):
        planes_start(k)
        side_copy(k).start()

    def halo_wait(k):
        @pl.when(gx > 0)
        def _():
            up_copy(k).wait_recv()

        @pl.when(gx < grid_x - 1)
        def _():
            down_copy(k).wait_recv()

        side_copy(k).wait_recv()

    def halo_sent(k):
        @pl.when(gx < grid_x - 1)
        def _():
            up_copy(k).wait_send()

        @pl.when(gx > 0)
        def _():
            down_copy(k).wait_send()

        side_copy(k).wait_send()

    over_partners(vox_copy, lambda c: c.start())
    for j in (1, 2):
        kid_copy(j).start()
    voxr[me] = slot_voxel[me]

    zero_plane = jnp.zeros((cy, cz), F32)

    @pl.when(gx == 0)
    def _():
        for k in range(5):
            vp[k, 0] = zero_plane

    @pl.when(gx == grid_x - 1)
    def _():
        for k in range(5):
            vp[k, cx + 1] = zero_plane

    def split_plane(i, c):
        high, low = pieces(c)
        at = pl.ds(pl.multiple_of(i * cy, cy), cy)
        xs[at, 0:cz] = high
        xs[at, cz : 2 * cz] = low

    def edge_row(c):
        return jnp.where(gy == 0, c[cy - 1 : cy, :], c[0:1, :])

    for n in range(4):
        loads[n].wait()

    def prepare(i, _):
        masked = gsb[i] * tmp_mask[i].astype(F32)
        vp[4, i + 1] = masked
        hys[4, pl.ds(i, 1), :] = edge_row(masked)
        c = vp[0, i + 1]
        hys[0, pl.ds(i, 1), :] = edge_row(c)
        split_plane(i, c)
        return 0

    lax.fori_loop(0, cx, prepare, 0)
    halo_start(0)
    halo_start(4)

    def cable_start(k):
        y = ys[k]
        turned = jnp.transpose(y)
        tails[k] = turned[N - 1 : N, :]
        heads[k] = turned[0:1, :]
        for c in cable_copies(k):
            c.start()
        high, low = pieces(y)
        yss[:, 0:N] = high
        yss[:, N : 2 * N] = low

    cable_start(0)
    chunks = S // LANES
    whose = lax.broadcasted_iota(jnp.int32, (LANES, 1), 0).astype(F32)
    has_parent = parent_row >= 0.0
    window = jnp.where(has_parent, parent_row - ((me - 2) * S).astype(F32), -1.0)
    window_high = jnp.floor(window * (1.0 / LANES))
    plt_s[...] = jnp.where(whose == window - window_high * LANES, 1.0, 0.0).astype(BF16)
    phm[...] = jnp.where(
        lax.broadcasted_iota(jnp.int32, phm.shape, 0).astype(F32) == window_high, 1.0, 0.0
    )
    sb[...] = jnp.transpose(jnp.broadcast_to(sigma_row[...], (LANES, S)))
    pgb[...] = jnp.zeros_like(pgb)
    pgr[...] = jnp.zeros_like(pgr)

    def build(width, depth, onehot, onehot_t, lane_mask, lane_mask_b, column):
        index = jnp.transpose(ta[...])[:cap, :]
        row = jnp.floor(index * (1.0 / width))
        lane = index - row * width
        lane_of = lax.broadcasted_iota(jnp.int32, (1, width), 1).astype(F32)
        row_of = lax.broadcasted_iota(jnp.int32, (1, depth), 1).astype(F32)
        for d in range(D):
            at = slice(d * cap, (d + 1) * cap)
            r = row[:, d : d + 1]
            onehot[at, :] = jnp.where(r == row_of, 1.0, 0.0).astype(BF16)
            hit = jnp.where(lane[:, d : d + 1] == lane_of, 1.0, 0.0)
            lane_mask[at, :] = hit
            lane_mask_b[at, :] = hit.astype(BF16)
            column[at, :] = jnp.broadcast_to(r, (cap, LANES))
        row_line = jnp.transpose(column[...])[0:1, :]
        step = 64

        def fill(b, _):
            ids = (lax.broadcasted_iota(jnp.int32, (step, 1), 0) + b * step).astype(F32)
            onehot_t[pl.ds(pl.multiple_of(b * step, step), step), :] = jnp.where(
                ids == row_line, 1.0, 0.0
            ).astype(BF16)
            return 0

        lax.fori_loop(0, depth // step, fill, 0)

    ta[...] = jnp.zeros_like(ta)
    ta[0:D, :] = slot_node
    build(N, S, op, opt, lmp, lmpb, colp)
    for j in (1, 2):
        kid_copy(j).wait_recv()
    kid_rows = [kids[...], kidr[0], kidr[1]]
    for w in range(3):
        cut = slice(w * S, (w + 1) * S)
        near = kid_rows[w][1:2, :] - (me * S).astype(F32)
        near_high = jnp.floor(near * (1.0 / LANES))
        hit = jnp.where(whose == near - near_high * LANES, 1.0, 0.0)
        kb[cut, :] = jnp.transpose(hit).astype(BF16)
        ids = lax.broadcasted_iota(jnp.int32, (khm.shape[0], 1), 0)
        ids = jnp.where(ids < chunks, ids, -1000000).astype(F32)
        khm[:, cut] = jnp.where(ids == near_high, 1.0, 0.0)
        kid_sigma[:, cut] = kid_rows[w][0:1, :]
    kid_total[...] = summed(dot(stacked_pieces(khm[...] * kid_sigma[...]), kb[...]))
    over_partners(vox_copy, lambda c: c.wait_recv())
    for d in range(D):
        ta[d : d + 1, :] = voxr[d]
    build(cz, rows, ot, ott, lm, lmb, colb)

    lane_id = lax.broadcasted_iota(jnp.int32, (1, LANES), 1)
    block = min(slots, 512)
    per_block = block // cap
    qt[...] = jnp.zeros_like(qt)
    qp[...] = jnp.zeros_like(qp)

    def gather(k):
        def step(b, carry):
            tissue, cable = carry
            at = pl.ds(pl.multiple_of(b * block, block), block)
            got = dot(ot[at, :], xs[...])
            got = (got[:, :cz] + got[:, cz:]) * lm[at, :]
            line = jnp.sum(got, axis=1, keepdims=True)
            gop = dot(op[at, :], yss[...])
            gop = (gop[:, :N] + gop[:, N:]) * lmp[at, :]
            linp = jnp.sum(gop, axis=1, keepdims=True)
            for j in range(per_block):
                here = lane_id == b * per_block + j
                tissue = jnp.where(here, line[j * cap : (j + 1) * cap], tissue)
                cable = jnp.where(here, linp[j * cap : (j + 1) * cap], cable)
            return tissue, cable

        zero = jnp.zeros((cap, LANES), F32)
        tissue, cable = lax.fori_loop(0, slots // block, step, (zero, zero))
        qt[0:cap, :] = tissue
        qp[0:cap, :] = cable
        turned_t = jnp.transpose(qt[...])
        turned_p = jnp.transpose(qp[...])
        for d in range(D):
            send[k, d, 0:1, :] = turned_p[d : d + 1, :]
            send[k, d, 1:2, :] = turned_t[d : d + 1, :]
        over_partners(functools.partial(junction_copy, k), lambda c: c.start())
        recv[k, me] = send[k, me]

    def currents(k):
        over_partners(functools.partial(junction_copy, k), lambda c: c.wait_recv())
        for d in range(D):
            ta[d : d + 1, :] = recv[k, d, 0:1, :]
            tb[d : d + 1, :] = recv[k, d, 1:2, :]
        rate = time_step * gap_conductance
        into_t = rate * (jnp.transpose(ta[...])[:cap, :] - qt[0:cap, :])
        into_p = rate * (qp[0:cap, :] - jnp.transpose(tb[...])[:cap, :])
        high_t, low_t = pieces(into_t)
        high_p, low_p = pieces(into_p)
        for d in range(D):
            at = slice(d * cap, (d + 1) * cap)
            ws[at, 0:cz] = high_t[:, d : d + 1] * lmb[at, :]
            ws[at, cz : 2 * cz] = low_t[:, d : d + 1] * lmb[at, :]
            wps[at, 0:N] = high_p[:, d : d + 1] * lmpb[at, :]
            wps[at, N : 2 * N] = low_p[:, d : d + 1] * lmpb[at, :]

    row_id = lax.broadcasted_iota(jnp.int32, (cy, 1), 0)
    z_id = lax.broadcasted_iota(jnp.int32, (1, cz), 1)

    def beside(k, i):
        c = vp[k, i + 1]
        side = hyr[k, pl.ds(i, 1), :]
        yp = jnp.where(row_id == cy - 1, side, pltpu.roll(c, cy - 1, 0))
        ym = jnp.where(row_id == 0, side, pltpu.roll(c, 1, 0))
        return c, (vp[k, i + 2], vp[k, i], yp, ym, pltpu.roll(c, cz - 1, 1), pltpu.roll(c, 1, 1))

    def weights(i):
        return (gxf[i + 1], gxf[i], gyp[i], gym[i], gzp[i], gzm[i])

    def face(a, b):
        return jnp.where(jnp.minimum(a, b) > 0.0, 0.5 * (a + b), 0.0)

    def faces(i, _):
        c = vp[4, i + 1]
        side = hyr[4, pl.ds(i, 1), :]
        below = jnp.where(gy > 0, side, 0.0)
        above = jnp.where(gy < grid_y - 1, side, 0.0)
        gxf[i] = face(vp[4, i], c)
        gyp[i] = face(c, jnp.where(row_id == cy - 1, above, pltpu.roll(c, cy - 1, 0)))
        gym[i] = face(c, jnp.where(row_id == 0, below, pltpu.roll(c, 1, 0)))
        gzp[i] = face(c, jnp.where(z_id == cz - 1, 0.0, pltpu.roll(c, cz - 1, 1)))
        gzm[i] = face(c, jnp.where(z_id == 0, 0.0, pltpu.roll(c, 1, 1)))
        return 0

    def cable(k, old, out):
        for c in cable_copies(k):
            c.wait_recv()
        tail_rows = [tailr[k, 1], tailr[k, 0], tails[k]]
        own_heads = heads[k]
        lines = [t[:, c * LANES : (c + 1) * LANES] for t in tail_rows for c in range(chunks)]
        pad = phm.shape[0] - len(lines)
        if pad:
            lines.append(jnp.zeros((pad, LANES), F32))
        found = summed(dot(stacked_pieces(jnp.concatenate(lines, axis=0)), plt_s[...]))
        parent_tail = jnp.sum(phm[...] * found, axis=0, keepdims=True)
        kid_heads = jnp.concatenate([own_heads, headr[k, 0], headr[k, 1]], axis=1)
        sums = summed(dot(stacked_pieces(khm[...] * (kid_sigma[...] * kid_heads)), kb[...]))
        inflow = jnp.concatenate(
            [
                sums[c : c + 1] - lines[2 * chunks + c] * kid_total[c : c + 1, :]
                for c in range(chunks)
            ],
            axis=1,
        )
        head = jnp.where(has_parent, sigma_row[...] * (parent_tail - own_heads), 0.0)
        place = lax.broadcasted_iota(jnp.int32, (N, 1), 0)
        ends[...] = jnp.transpose(
            jnp.where(place == 0, head, 0.0) + jnp.where(place == N - 1, inflow, 0.0)
        )
        if old is None:
            ptr[k] = parent_tail
        else:
            over = (own_heads - parent_tail) * (ptr[old] - heads[old])
            pgr[...] = pgr[...] + time_step * jnp.where(has_parent, over, 0.0)
        step = min(S, 256)
        node = lax.broadcasted_iota(jnp.int32, (1, N), 1)

        def part(b, _):
            at = pl.ds(pl.multiple_of(b * step, step), step)
            y = ys[k, at, :]
            step_up = jnp.where(node < N - 1, pltpu.roll(y, N - 1, 1) - y, 0.0)
            edge = sb[at, :] * step_up
            flux = edge - pltpu.roll(edge, 1, 1) + ends[at, :]
            if old is None:
                out[at, :] = y + time_step * (flux + ionic(y))
            else:
                u = ys[old, at, :]
                rise = jnp.where(node < N - 1, pltpu.roll(u, N - 1, 1) - u, 0.0)
                pgb[at, :] = pgb[at, :] - time_step * (step_up * rise)
                out[at, :] = y + time_step * (flux + slope(u) * y)
            return 0

        lax.fori_loop(0, S // step, part, 0)

    group = 4 if cx % 4 == 0 else 1

    def spread(finish, between=None):
        def step(b):
            at = pl.ds(pl.multiple_of(b * (group * cy), group * cy), group * cy)
            add = dot(ott[at, :], ws[...])
            add = add[:, :cz] + add[:, cz:]
            for g in range(group):
                finish(b * group + g, add[g * cy : (g + 1) * cy])

        groups = cx // group

        def outer(b, _):
            step(b * (groups - 1))
            return 0

        def inner(b, _):
            step(b)
            return 0

        lax.fori_loop(0, 2, outer, 0)
        if between is not None:
            planes_start(between)
        lax.fori_loop(1, groups - 1, inner, 0)
        if between is not None:
            side_copy(between).start()

    def spread_cable():
        add = dot(opt[...], wps[...])
        return add[:, :N] + add[:, N:]

    for k in range(2):
        gather(k)
        if k == 0:
            halo_wait(4)
            lax.fori_loop(0, cx, faces, 0)
            gxf[cx] = face(vp[4, cx], vp[4, cx + 1])
        halo_wait(k)

        def forward(i, _, k=k):
            c, others = beside(k, i)
            total = zero_plane
            for g, n in zip(weights(i), others):
                total = total + g * (n - c)
            new = c + time_step * (total + ionic(c))
            if k == 0:
                vp[1, i + 1] = new
            else:
                v2b[i] = new
            return 0

        lax.fori_loop(0, cx, forward, 0)
        out = ys.at[1] if k == 0 else y2b
        cable(k, None, out)
        currents(k)
        out[...] = out[...] - spread_cable()
        if k == 0:
            def finish(i, add):
                new = vp[1, i + 1] + add
                vp[1, i + 1] = new
                hys[1, pl.ds(i, 1), :] = edge_row(new)
                split_plane(i, new)
        else:
            loads[4].wait()
            loads[5].wait()
            ys[2] = loss_weight * (y2b[...] - (1.0 - ptarget[...].astype(F32) / target_span))

            def finish(i, add):
                new = v2b[i] + add
                v2b[i] = new
                goal = 1.0 - target[i].astype(F32) / target_span
                seed = jnp.where(vp[4, i + 1] > 0.0, loss_weight * (new - goal), 0.0)
                vp[2, i + 1] = seed
                hys[2, pl.ds(i, 1), :] = edge_row(seed)
                split_plane(i, seed)
        cable_start(k + 1)
        spread(finish, k + 1)

    stores = [
        pltpu.make_async_copy(v2b, v2_o, loc_sem.at[6]),
        pltpu.make_async_copy(y2b, y2_o, loc_sem.at[7]),
    ]
    for c in stores:
        c.start()

    for k in (2, 3):
        old = 3 - k
        gather(k)
        halo_wait(k)

        def backward(i, _, k=k, old=old):
            c, others = beside(k, i)
            v, befores = beside(old, i)
            total = zero_plane
            grad = zero_plane
            for g, n, b in zip(weights(i), others, befores):
                d = n - c
                total = total + g * d
                grad = grad + jnp.where(g > 0.0, d * (v - b), 0.0)
            new = c + time_step * (total + slope(v) * c)
            grad = (0.5 * time_step) * grad
            if k == 2:
                vp[3, i + 1] = new
                gsb[i] = grad
            else:
                l0b[i] = new
                gsb[i] = gsb[i] + grad
            return 0

        lax.fori_loop(0, cx, backward, 0)
        out = ys.at[3] if k == 2 else mu0b
        cable(k, old, out)
        currents(k)
        out[...] = out[...] - spread_cable()
        if k == 2:
            cable_start(3)

            def finish(i, add):
                new = vp[3, i + 1] + add
                vp[3, i + 1] = new
                hys[3, pl.ds(i, 1), :] = edge_row(new)
                split_plane(i, new)
        else:
            stores.append(pltpu.make_async_copy(gsb, gs_o, loc_sem.at[8]))
            stores[-1].start()
            stores.append(pltpu.make_async_copy(mu0b, mu_o, loc_sem.at[9]))
            stores[-1].start()
            gp_o[...] = pgr[...] + jnp.sum(jnp.transpose(pgb[...]), axis=0, keepdims=True)

            def finish(i, add):
                l0b[i] = l0b[i] + add
        spread(finish, 3 if k == 2 else None)

    stores.append(pltpu.make_async_copy(l0b, la_o, loc_sem.at[10]))
    stores[-1].start()
    over_partners(vox_copy, lambda c: c.wait_send())
    for j in (1, 2):
        kid_copy(j).wait_send()
    for k in range(5):
        halo_sent(k)
    for k in range(4):
        over_partners(functools.partial(junction_copy, k), lambda c: c.wait_send())
        for c in cable_copies(k):
            c.wait_send()
    for c in stores:
        c.wait()


def put_out(*refs):
    n = (len(refs) - 1) // 2
    copies = [pltpu.make_async_copy(refs[i], refs[n + i], refs[-1].at[i]) for i in range(n)]
    for c in copies:
        c.start()
    for c in copies:
        c.wait()


def body(
    initial_voltage, conductivity, tissue_mask, target_step, initial_purkinje,
    purkinje_conductivity, segment_parent, purkinje_target, junction_voxel, junction_node,
):
    cx, cy, cz = initial_voltage.shape
    S, N = initial_purkinje.shape
    grid_x = lax.axis_size("gx")
    grid_y = lax.axis_size("gy")
    assert grid_y == 2 and N == LANES
    D = grid_x * grid_y
    per_device = junction_voxel.shape[0]
    cap = max(16, 2 * per_device // D)
    assert cap <= LANES and D <= LANES
    slots = D * cap
    rows = cx * cy

    chunks = S // LANES
    window_rows = -(-3 * chunks // 16) * 16
    kid_rows = -(-chunks // 16) * 16

    any_spec = pl.BlockSpec(memory_space=pl.ANY)
    vmem = pl.BlockSpec(memory_space=pltpu.VMEM)
    hbm = pl.BlockSpec(memory_space=pltpu.HBM)
    V = pltpu.VMEM
    dma = pltpu.SemaphoreType.DMA
    field = V((cx, cy, cz), F32)
    fibre = V((S, N), F32)
    scratch = [
        V((5, cx + 2, cy, cz), F32), V((5, cx, cz), F32), V((5, cx, cz), F32),
        V((cx, cy, cz), jnp.int32), V((cx, cy, cz), jnp.int32), V((cx + 1, cy, cz), F32),
        field, field, field, field, field, field, field,
        V((4, S, N), F32), fibre, fibre, V((S, N), jnp.int32), V((S, LANES), F32),
        fibre, fibre, V((1, S), F32), V((2, 1, S), F32), V((LANES, S), BF16), V((window_rows, S), F32),
        V((3 * S, LANES), BF16), V((kid_rows, 3 * S), F32), V((1, 3 * S), F32), V((kid_rows, LANES), F32),
        V((slots, rows), BF16), V((rows, slots), BF16), V((slots, cz), F32), V((slots, cz), BF16),
        V((rows, 2 * cz), BF16), V((slots, 2 * cz), BF16),
        V((slots, S), BF16), V((S, slots), BF16), V((slots, N), F32), V((slots, N), BF16),
        V((S, 2 * N), BF16), V((slots, 2 * N), BF16), V((D, 1, LANES), F32),
        V((LANES, LANES), F32), V((LANES, LANES), F32), V((LANES, LANES), F32),
        V((LANES, LANES), F32), V((slots, LANES), F32), V((slots, LANES), F32),
        V((4, D, 2, LANES), F32), V((4, D, 2, LANES), F32), V((D, 1, LANES), F32),
        V((4, 1, S), F32), V((4, 1, S), F32), V((4, 2, 1, S), F32), V((4, 2, 1, S), F32),
        V((2, S), F32), V((2, 2, S), F32),
        dma((11,)), dma((4, D)), dma((4, D)), dma((D,)), dma((D,)),
        dma((5, 2)), dma((5, 2)), dma((5,)), dma((5,)), dma((4, 4)), dma((4, 4)),
        dma((2,)), dma((2,)),
    ]
    tissue = jax.ShapeDtypeStruct((cx, cy, cz), F32)
    cable = jax.ShapeDtypeStruct((S, N), F32)
    v2, y2, gs, gp, la, mu = pl.pallas_call(
        functools.partial(kernel, grid_x, grid_y, cap),
        name="monodomain",
        out_shape=(tissue, cable, tissue, jax.ShapeDtypeStruct((1, S), F32), tissue, cable),
        in_specs=[hbm] * 5 + [vmem] * 2 + [hbm] + [vmem] * 2,
        out_specs=(any_spec, any_spec, any_spec, vmem, any_spec, any_spec),
        scratch_shapes=scratch,
        compiler_params=pltpu.CompilerParams(
            collective_id=0, has_side_effects=True, vmem_limit_bytes=36 * 1024 * 1024
        ),
    )(
        *[pltpu.with_memory_space_constraint(a, pltpu.HBM) for a in (
            initial_voltage, conductivity, tissue_mask, target_step, initial_purkinje)],
        purkinje_conductivity.reshape(1, S), segment_parent.reshape(1, S),
        pltpu.with_memory_space_constraint(purkinje_target, pltpu.HBM), junction_voxel.reshape(1, per_device), junction_node.reshape(1, per_device),
    )
    results = (v2, y2, gs, gp, la, mu)
    v2, y2, gs, gp, la, mu = pl.pallas_call(
        put_out,
        name="put_out",
        out_shape=tuple(jax.ShapeDtypeStruct(r.shape, r.dtype) for r in results),
        in_specs=[any_spec] * 6,
        out_specs=(hbm,) * 6,
        scratch_shapes=[dma((6,))],
        compiler_params=pltpu.CompilerParams(vmem_limit_bytes=1024 * 1024),
    )(*results)
    return v2, y2, gs, gp.reshape(S), la, mu


def solution(mesh):
    tissue = P(("groups", "gx"), "gy", None)
    cable = P(("groups", "gx", "gy"), None)
    line = P(("groups", "gx", "gy"))
    return jax.shard_map(
        body,
        mesh=mesh,
        in_specs=(tissue, tissue, tissue, tissue, cable, line, line, cable, line, line),
        out_specs=(tissue, cable, tissue, line, tissue, cable),
        check_vma=False,
    )
```
